256 devices in a mesh: row: 16 (over y_lo, x, core), col: 16 (over y_hi, z).
Axes of the slice: x: 4, y: 4 (y_hi: 2, y_lo: 2; y = y_hi * 2 + y_lo), z: 8, core: 2. Of those that a mesh axis runs over, the one named last changes fastest.
Arguments:
- tokens: bfloat16 [512, 12288], P('row', 'col'), may hold values from -6 to 6
- out_grad: bfloat16 [512, 12288], P('row', 'col'), may hold values from -6 to 6
- w_in: bfloat16 [12288, 24576], P('col', 'row'), may hold values from -0.0546875 to 0.0546875
- w_out: bfloat16 [24576, 12288], P('row', 'col'), may hold values from -0.0390625 to 0.0390625
- bias_in: float32 [24576], P('row'), may hold values from -3 to 3
- stream_ids: int32 [3], replicated, may hold values from 0 to 4095
- tile_keys: int32 [64, 192], replicated, may hold values from 0 to 16777215
Outputs:
- grad_tokens: bfloat16 [512, 12288], P('row', 'col')
- grad_w_in: bfloat16 [12288, 24576], P('col', 'row')
- grad_w_out: bfloat16 [24576, 12288], P('row', 'col')
- grad_bias_in: float32 [24576], P('row')
- grad_bias_out: float32 [12288], P('col')
The draws below stay inside these ranges and needn't reach their ends.
All inputs are finite; a program needn't handle non-finite values.
Results may differ from the reference program's by a relative error of at most 0.005.
Values may be sent and summed in bfloat16 or wider, within the bound.
No kernel may reach another device: no remote copies, remote signals or barrier semaphores. Data moves between devices by JAX's collectives and lax.ppermute only.
A program may use at most 64 MiB of HBM per device.

```python
import jax
import jax.numpy as jnp
from jax import lax

D = 12288
FF = 24576
TOKENS = 512
TILE_T = 8
TILE_F = 128


def with_ends(result, stream_key, low, high):
    longest = result.shape.index(max(result.shape))
    spots = []
    for shift in (0, 1):
        where = [jax.random.randint(jax.random.fold_in(stream_key, axis), (), 0, length) for axis, length in enumerate(result.shape)]
        where[longest] = (where[longest] + shift) % result.shape[longest]
        spots.append(tuple(where))
    return result.at[spots[0]].set(low).at[spots[1]].set(high)


def levels(own_key, extent, pieces, least, high):
    level = 1.0
    for position, parts in pieces:
        heights = jax.random.uniform(jax.random.fold_in(jax.random.fold_in(own_key, 6), position), (parts,), jnp.float32, least / len(pieces), high / len(pieces))
        level = level * jnp.repeat(jnp.exp(heights), extent[position] // parts).reshape((-1,) + (1,) * (len(extent) - 1 - position))
    return level


def gaussian(rng, shape, scale, limit, shards=(), kind=jnp.bfloat16):
    result = jax.random.normal(rng, shape, jnp.float32) * scale
    if len(shards) > 0:
        result = levels(rng, shape, shards, -0.22, 0.18) * result
    return jnp.clip(result, min=-limit, max=limit).astype(kind)


def setup_inputs(seed: int = 0) -> dict:
    splits = jax.random.split(jax.random.key(seed), 8)
    tokens = gaussian(splits[0], (TOKENS, D), 1.0, 6.0, ((0, 16), (1, 16)))
    out_grad = gaussian(splits[1], (TOKENS, D), 1.0, 6.0, ((0, 16), (1, 16)))
    w_in = gaussian(splits[2], (D, FF), D ** -0.5, 0.0546875, ((0, 16), (1, 16)))
    w_out = gaussian(splits[3], (FF, D), FF ** -0.5, 0.0390625, ((0, 16), (1, 16)))
    bias_in = gaussian(splits[4], (FF,), 0.5, 3.0, ((0, 16),), jnp.float32)
    stream_ids = jax.random.randint(splits[5], (3,), 0, 4096).astype(jnp.int32)
    tile_keys = with_ends(jax.random.randint(splits[6], (TOKENS // TILE_T, FF // TILE_F), 0, 16777216), jax.random.fold_in(splits[6], 1), 0, 16777215).astype(jnp.int32)
    return {"tokens": tokens, "out_grad": out_grad, "w_in": w_in, "w_out": w_out, "bias_in": bias_in, "stream_ids": stream_ids, "tile_keys": tile_keys}


mix_one = 73856093
mix_two = 19349663
mix_three = 83492791
golden = -1640531535
mult_one = 2146121005
mult_two = -2073254261


def shift_down(value, count):
    return lax.shift_right_logical(value, jnp.full(value.shape, count, jnp.int32))


def keep_mask(tile_keys, stream_ids, row_start, row_count, col_start, col_count, tile_t, tile_f):
    row_ids = row_start + jnp.arange(row_count, dtype=jnp.int32)
    col_ids = col_start + jnp.arange(col_count, dtype=jnp.int32)
    onehot_rows = (row_ids[:, None] // tile_t == jnp.arange(tile_keys.shape[0], dtype=jnp.int32)[None, :]).astype(jnp.int32)
    onehot_cols = (jnp.arange(tile_keys.shape[1], dtype=jnp.int32)[:, None] == col_ids[None, :] // tile_f).astype(jnp.int32)
    picked = jnp.dot(onehot_rows, tile_keys, preferred_element_type=jnp.int32)
    picked = jnp.dot(picked, onehot_cols, preferred_element_type=jnp.int32)
    salt = (stream_ids[0] * jnp.int32(mix_one)) ^ (stream_ids[1] * jnp.int32(mix_two)) ^ (stream_ids[2] * jnp.int32(mix_three))
    offset = (row_ids[:, None] % tile_t) * tile_f + col_ids[None, :] % tile_f
    value = (picked ^ salt) + offset * jnp.int32(golden)
    value = value ^ shift_down(value, 16)
    value = value * jnp.int32(mult_one)
    value = value ^ shift_down(value, 15)
    value = value * jnp.int32(mult_two)
    value = value ^ shift_down(value, 16)
    return ((shift_down(value, 8) & jnp.int32(1023)) < jnp.int32(922)).astype(jnp.float32)


def normal_cdf(value):
    return 0.5 * (1.0 + lax.erf(value * 0.7071067811865476))


def reference(tokens, out_grad, w_in, w_out, bias_in, stream_ids, tile_keys):
    pre = jnp.dot(tokens, w_in, preferred_element_type=jnp.float32) + bias_in.astype(jnp.float32)
    keep = keep_mask(tile_keys, stream_ids, 0, TOKENS, 0, FF, TILE_T, TILE_F)
    scaled = keep * (1.0 / 0.9)
    cdf = normal_cdf(pre)
    act = (pre * cdf * scaled).astype(jnp.bfloat16)
    dact = lax.dot_general(out_grad, w_out, (((1,), (1,)), ((), ())), preferred_element_type=jnp.float32)
    slope = cdf + pre * jnp.exp(-0.5 * pre * pre) * 0.3989422804014327
    dpre = (dact * scaled * slope).astype(jnp.bfloat16)
    grad_w_out = lax.dot_general(act, out_grad, (((0,), (0,)), ((), ())), preferred_element_type=jnp.float32).astype(jnp.bfloat16)
    grad_w_in = lax.dot_general(tokens, dpre, (((0,), (0,)), ((), ())), preferred_element_type=jnp.float32).astype(jnp.bfloat16)
    grad_tokens = lax.dot_general(dpre, w_in, (((1,), (1,)), ((), ())), preferred_element_type=jnp.float32).astype(jnp.bfloat16)
    grad_bias_in = jnp.sum(dpre.astype(jnp.float32), axis=0)
    grad_bias_out = jnp.sum(out_grad.astype(jnp.float32), axis=0)
    return (grad_tokens, grad_w_in, grad_w_out, grad_bias_in, grad_bias_out)
```

```python
import jax
import jax.numpy as jnp
from jax import lax
from jax.experimental import pallas as pl
from jax.experimental.pallas import tpu as pltpu
from jax.sharding import PartitionSpec as P

TILE_T = 8
TILE_F = 128
RING = 8

mix_one = 73856093
mix_two = 19349663
mix_three = 83492791
golden = -1640531535
mult_one = 2146121005
mult_two = -2073254261

f32 = jnp.float32
bf16 = jnp.bfloat16


def shift_down(value, count):
    return lax.shift_right_logical(value, jnp.full(value.shape, count, jnp.int32))


def keep_mask(tile_keys, stream_ids, row_ids, col_ids, tile_t, tile_f):
    onehot_rows = (
        row_ids[:, None] // tile_t == jnp.arange(tile_keys.shape[0], dtype=jnp.int32)[None, :]
    ).astype(jnp.int32)
    onehot_cols = (
        jnp.arange(tile_keys.shape[1], dtype=jnp.int32)[:, None] == col_ids[None, :] // tile_f
    ).astype(jnp.int32)
    picked = jnp.dot(onehot_rows, tile_keys, preferred_element_type=jnp.int32)
    picked = jnp.dot(picked, onehot_cols, preferred_element_type=jnp.int32)
    salt = (
        stream_ids[0] * jnp.int32(mix_one)
        ^ stream_ids[1] * jnp.int32(mix_two)
        ^ stream_ids[2] * jnp.int32(mix_three)
    )
    offset = row_ids[:, None] % tile_t * tile_f + col_ids[None, :] % tile_f
    value = (picked ^ salt) + offset * jnp.int32(golden)
    value = value ^ shift_down(value, 16)
    value = value * jnp.int32(mult_one)
    value = value ^ shift_down(value, 15)
    value = value * jnp.int32(mult_two)
    value = value ^ shift_down(value, 16)
    return (shift_down(value, 8) & jnp.int32(1023) < jnp.int32(922)).astype(f32)


def normal_cdf(value):
    return 0.5 * (1.0 + lax.erf(value * 0.7071067811865476))


def local_gelu(pre, dact, keep):
    scaled = keep * (1.0 / 0.9)
    cdf = normal_cdf(pre)
    act = (pre * cdf * scaled).astype(bf16)
    slope = cdf + pre * jnp.exp(-0.5 * pre * pre) * 0.3989422804014327
    dpre = (dact * scaled * slope).astype(bf16)
    return act, dpre


def row_xor(value, bits):
    return lax.ppermute(value, "row", [(i, i ^ bits) for i in range(16)])


def near_swap(value):
    return lax.ppermute(value, "col", [(i, i ^ 1) for i in range(16)])


def next_swap(value):
    pairs = []
    for y in range(2):
        for z in range(RING):
            pairs.append((y * RING + z, y * RING + (z + (1 if z % 2 else -1)) % RING))
    return lax.ppermute(value, "col", pairs)


def far_swap(value):
    return lax.ppermute(value, "col", [(i, i ^ 8) for i in range(16)])


def encode(value):
    root = jnp.sqrt(jnp.abs(value) * 262144.0)
    return jnp.where(value < 0, -root, root).astype(jnp.float16)


def decode(code):
    root = code.astype(f32)
    return root * jnp.abs(root) * (1.0 / 262144.0)


def ring_reduce(part):
    half = part(4)
    mid = half.shape[0] // 2
    near = near_swap(encode(half[:mid]))
    back = next_swap(encode(half[mid:]))
    own = part(5)
    to_next = jnp.concatenate([own[:mid] + decode(near), own[mid:]], 0)
    own = part(3)
    to_near = jnp.concatenate([own[:mid], own[mid:] + decode(back)], 0)
    for k in (2, 1):
        near = near_swap(encode(to_near))
        back = next_swap(encode(to_next))
        to_next = part(8 - k) + decode(near)
        to_near = part(k) + decode(back)
    near = near_swap(encode(to_near))
    back = next_swap(encode(to_next))
    return part(0) + decode(near) + decode(back)


def ring_gather(own):
    mid = own.shape[0] // 2
    chunks = [own] + [None] * 7
    near = back = own
    for k in (1, 2, 3):
        near, back = next_swap(near), near_swap(back)
        chunks[k] = back
        chunks[8 - k] = near
        near, back = back, near
    near, back = near_swap(back[:mid]), next_swap(near[mid:])
    chunks[4] = jnp.concatenate([near, back], 0)
    return jnp.concatenate(chunks, 0)


VMEM = pl.BlockSpec(memory_space=pltpu.VMEM)
SMEM = pl.BlockSpec(memory_space=pltpu.SMEM)


def stack_body(*refs):
    for e in range(8):
        refs[8][e] = refs[e][...]


def ring_place(chip_bits, place):
    ahead = chip_bits - place
    return jnp.where(place % 2 == 0, ahead, -ahead) & 7


def place_body(where, mine, other, out):
    height = mine.shape[1]
    for e in range(8):
        k = where[e]
        out[k, :height] = mine[e]
        out[k, height:] = other[e]


def unplace_body(where, part, mine, other):
    height = mine.shape[1]
    for e in range(8):
        k = where[e]
        mine[e] = part[k, :height]
        other[e] = part[k, height:]


def gather_rows(shard, where):
    height, width = shard.shape
    pieces = [shard] + [row_xor(shard, 2 * e) for e in range(1, 8)]
    mine = pl.pallas_call(
        stack_body,
        out_shape=jax.ShapeDtypeStruct((8, height, width), shard.dtype),
        in_specs=[VMEM] * 8,
        out_specs=VMEM,
    )(*pieces)
    other = row_xor(mine, 1)
    whole = pl.pallas_call(
        place_body,
        out_shape=jax.ShapeDtypeStruct((8, 2 * height, width), shard.dtype),
        in_specs=[SMEM, VMEM, VMEM],
        out_specs=VMEM,
    )(where, mine, other)
    return whole.reshape(16 * height, width), other


def local(tokens, out_grad, w_in, w_out, bias_in, stream_ids, tile_keys):
    row = lax.axis_index("row")
    col = lax.axis_index("col")
    chip = row // 2
    core = row % 2
    z = col % RING
    ff = w_in.shape[1]
    width = w_in.shape[0]
    height = tokens.shape[0]
    eight = jnp.arange(8, dtype=jnp.int32)

    toks, gate = gather_rows(tokens, ring_place(eight, z))
    out_grad, gate = lax.optimization_barrier((out_grad, gate))
    grads, _ = gather_rows(out_grad, ring_place(eight, z))

    pre_terms = jnp.dot(toks, w_in, preferred_element_type=f32)
    dact_terms = lax.dot_general(
        grads, w_out, (((1,), (1,)), ((), ())), preferred_element_type=f32
    )

    def reduced(terms):
        total = ring_reduce(lambda k: terms[64 * k : 64 * k + 64])
        code = encode(total)
        code, peer = lax.optimization_barrier((code, far_swap(code)))
        return decode(code) + decode(peer)

    pre = reduced(pre_terms) + bias_in[None, :]
    dact = reduced(dact_terms)

    place = jnp.arange(2 * height, dtype=jnp.int32)
    row_ids = (chip ^ z) * (2 * height) + (place // height ^ core) * height + place % height
    col_ids = row * ff + jnp.arange(ff, dtype=jnp.int32)
    keep = keep_mask(tile_keys, stream_ids, row_ids, col_ids, TILE_T, TILE_F)
    act, dpre = local_gelu(pre, dact, keep)

    dpre_all = ring_gather(dpre)
    act_all = ring_gather(act)

    part = lax.dot_general(
        dpre_all, w_in, (((1,), (1,)), ((), ())), preferred_element_type=f32
    ).reshape(8, 2 * height, width)
    half = jax.ShapeDtypeStruct((8, height, width), f32)
    mine, other = pl.pallas_call(
        unplace_body,
        out_shape=(half, half),
        in_specs=[SMEM, VMEM],
        out_specs=(VMEM, VMEM),
    )(ring_place(eight ^ chip, z), part)
    sums = (mine + row_xor(other, 1)).astype(bf16)
    sums = lax.all_to_all(
        sums,
        "row",
        0,
        0,
        axis_index_groups=[[2 * q + c for q in range(8)] for c in range(2)],
        tiled=True,
    )
    grad_tokens = jnp.sum(sums.astype(f32), axis=0).astype(bf16)

    grad_w_in = lax.dot_general(
        toks, dpre_all, (((0,), (0,)), ((), ())), preferred_element_type=f32
    ).astype(bf16)
    grad_w_out = lax.dot_general(
        act_all, grads, (((0,), (0,)), ((), ())), preferred_element_type=f32
    ).astype(bf16)

    def ordered(sums, index):
        return jnp.sum(jnp.take(sums, index, axis=0), axis=0)

    grad_bias_in = ordered(
        jnp.sum(dpre_all.astype(f32).reshape(8, 64, ff), axis=1), ring_place(eight, z)
    )
    rows = jnp.arange(16, dtype=jnp.int32)
    rows = ring_place(rows // 2 ^ chip, z) * 2 + (rows % 2 ^ core)
    grad_bias_out = ordered(jnp.sum(grads.astype(f32).reshape(16, height, width), axis=1), rows)
    return (grad_tokens, grad_w_in, grad_w_out, grad_bias_in, grad_bias_out)


def solution(mesh):
    return jax.shard_map(
        local,
        mesh=mesh,
        in_specs=(
            P("row", "col"),
            P("row", "col"),
            P("col", "row"),
            P("row", "col"),
            P("row"),
            P(),
            P(),
        ),
        out_specs=(P("row", "col"), P("col", "row"), P("row", "col"), P("row"), P("col")),
        check_vma=False,
    )
```

```python
import jax
import jax.numpy as jnp
from jax import lax
from jax.sharding import PartitionSpec as P

TILE_T = 8
TILE_F = 128
RING = 8

mix_one = 73856093
mix_two = 19349663
mix_three = 83492791
golden = -1640531535
mult_one = 2146121005
mult_two = -2073254261

f32 = jnp.float32
bf16 = jnp.bfloat16


def shift_down(value, count):
    return lax.shift_right_logical(value, jnp.full(value.shape, count, jnp.int32))


def keep_mask(tile_keys, stream_ids, row_ids, col_ids, tile_t, tile_f):
    onehot_rows = (
        row_ids[:, None] // tile_t == jnp.arange(tile_keys.shape[0], dtype=jnp.int32)[None, :]
    ).astype(jnp.int32)
    onehot_cols = (
        jnp.arange(tile_keys.shape[1], dtype=jnp.int32)[:, None] == col_ids[None, :] // tile_f
    ).astype(jnp.int32)
    picked = jnp.dot(onehot_rows, tile_keys, preferred_element_type=jnp.int32)
    picked = jnp.dot(picked, onehot_cols, preferred_element_type=jnp.int32)
    salt = (
        stream_ids[0] * jnp.int32(mix_one)
        ^ stream_ids[1] * jnp.int32(mix_two)
        ^ stream_ids[2] * jnp.int32(mix_three)
    )
    offset = row_ids[:, None] % tile_t * tile_f + col_ids[None, :] % tile_f
    value = (picked ^ salt) + offset * jnp.int32(golden)
    value = value ^ shift_down(value, 16)
    value = value * jnp.int32(mult_one)
    value = value ^ shift_down(value, 15)
    value = value * jnp.int32(mult_two)
    value = value ^ shift_down(value, 16)
    return (shift_down(value, 8) & jnp.int32(1023) < jnp.int32(922)).astype(f32)


def normal_cdf(value):
    return 0.5 * (1.0 + lax.erf(value * 0.7071067811865476))


def local_gelu(pre, dact, keep):
    scaled = keep * (1.0 / 0.9)
    cdf = normal_cdf(pre)
    act = (pre * cdf * scaled).astype(bf16)
    slope = cdf + pre * jnp.exp(-0.5 * pre * pre) * 0.3989422804014327
    dpre = (dact * scaled * slope).astype(bf16)
    return act, dpre


def near_swap(value):
    return lax.ppermute(value, "col", [(i, i ^ 1) for i in range(16)])


def next_swap(value):
    pairs = []
    for y in range(2):
        for z in range(RING):
            pairs.append((y * RING + z, y * RING + (z + (1 if z % 2 else -1)) % RING))
    return lax.ppermute(value, "col", pairs)


def far_swap(value):
    return lax.ppermute(value, "col", [(i, i ^ 8) for i in range(16)])


def encode(value):
    root = jnp.sqrt(jnp.abs(value) * 262144.0)
    return jnp.where(value < 0, -root, root).astype(jnp.float16)


def decode(code):
    root = code.astype(f32)
    return root * jnp.abs(root) * (1.0 / 262144.0)


def ring_reduce(part):
    half = part(4)
    mid = half.shape[0] // 2
    near = near_swap(encode(half[:mid]))
    back = next_swap(encode(half[mid:]))
    own = part(5)
    to_next = jnp.concatenate([own[:mid] + decode(near), own[mid:]], 0)
    own = part(3)
    to_near = jnp.concatenate([own[:mid], own[mid:] + decode(back)], 0)
    for k in (2, 1):
        near = near_swap(encode(to_near))
        back = next_swap(encode(to_next))
        to_next = part(8 - k) + decode(near)
        to_near = part(k) + decode(back)
    near = near_swap(encode(to_near))
    back = next_swap(encode(to_next))
    return part(0) + decode(near) + decode(back)


def ring_gather(own, spot):
    height, width = own.shape
    mid = height // 2
    whole = jnp.zeros((8 * height, width), own.dtype)

    def put(whole, chunk, start):
        return lax.dynamic_update_slice(whole, chunk, (start, 0))

    whole = put(whole, own, spot(0))
    near = back = own
    for k in (1, 2, 3):
        near, back = next_swap(near), near_swap(back)
        whole = put(put(whole, back, spot(k)), near, spot(8 - k))
        near, back = back, near
    near, back = near_swap(back[:mid]), next_swap(near[mid:])
    return put(put(whole, near, spot(4)), back, spot(4) + mid)


def row_gather(shard):
    whole = jnp.broadcast_to(shard[None], (16,) + shard.shape)
    whole = lax.all_to_all(whole, "row", 0, 0, tiled=True)
    return whole.reshape(16 * shard.shape[0], shard.shape[1])


def local(tokens, out_grad, w_in, w_out, bias_in, stream_ids, tile_keys):
    row = lax.axis_index("row")
    col = lax.axis_index("col")
    z = col % RING
    ff = w_in.shape[1]
    width = w_in.shape[0]
    height = tokens.shape[0]
    ahead = jnp.where(z % 2 == 0, 1, -1)

    def spot(k):
        return (z + ahead * k) % RING * (2 * height)

    toks = row_gather(tokens)
    out_grad, toks = lax.optimization_barrier((out_grad, toks))
    grads = row_gather(out_grad)

    pre_terms = jnp.dot(toks, w_in, preferred_element_type=f32)
    dact_terms = lax.dot_general(
        grads, w_out, (((1,), (1,)), ((), ())), preferred_element_type=f32
    )

    def reduced(terms):
        total = ring_reduce(lambda k: lax.dynamic_slice_in_dim(terms, spot(k), 2 * height, 0))
        code = encode(total)
        code, peer = lax.optimization_barrier((code, far_swap(code)))
        return decode(code) + decode(peer)

    pre = reduced(pre_terms) + bias_in[None, :]
    dact = reduced(dact_terms)

    row_ids = spot(0) + jnp.arange(2 * height, dtype=jnp.int32)
    col_ids = row * ff + jnp.arange(ff, dtype=jnp.int32)
    keep = keep_mask(tile_keys, stream_ids, row_ids, col_ids, TILE_T, TILE_F)
    act, dpre = local_gelu(pre, dact, keep)

    dpre_all = ring_gather(dpre, spot)
    act_all = ring_gather(act, spot)

    part = lax.dot_general(
        dpre_all, w_in, (((1,), (1,)), ((), ())), preferred_element_type=f32
    ).astype(bf16)
    part = lax.all_to_all(part.reshape(16, height, width), "row", 0, 0, tiled=True)
    grad_tokens = jnp.sum(part.astype(f32), axis=0).astype(bf16)

    grad_w_in = lax.dot_general(
        toks, dpre_all, (((0,), (0,)), ((), ())), preferred_element_type=f32
    ).astype(bf16)
    grad_w_out = lax.dot_general(
        act_all, grads, (((0,), (0,)), ((), ())), preferred_element_type=f32
    ).astype(bf16)
    grad_bias_in = jnp.sum(dpre_all.astype(f32), axis=0)
    grad_bias_out = jnp.sum(grads.astype(f32), axis=0)
    return (grad_tokens, grad_w_in, grad_w_out, grad_bias_in, grad_bias_out)


def solution(mesh):
    return jax.shard_map(
        local,
        mesh=mesh,
        in_specs=(
            P("row", "col"),
            P("row", "col"),
            P("col", "row"),
            P("row", "col"),
            P("row"),
            P(),
            P(),
        ),
        out_specs=(P("row", "col"), P("col", "row"), P("row", "col"), P("row"), P("col")),
        check_vma=False,
    )
```

```python
import jax
import jax.numpy as jnp
from jax import lax
from jax.sharding import PartitionSpec as P

TILE_T = 8
TILE_F = 128
RING = 8

mix_one = 73856093
mix_two = 19349663
mix_three = 83492791
golden = -1640531535
mult_one = 2146121005
mult_two = -2073254261

f32 = jnp.float32
bf16 = jnp.bfloat16


def shift_down(value, count):
    return lax.shift_right_logical(value, jnp.full(value.shape, count, jnp.int32))


def keep_mask(tile_keys, stream_ids, row_ids, col_ids, tile_t, tile_f):
    onehot_rows = (
        row_ids[:, None] // tile_t == jnp.arange(tile_keys.shape[0], dtype=jnp.int32)[None, :]
    ).astype(jnp.int32)
    onehot_cols = (
        jnp.arange(tile_keys.shape[1], dtype=jnp.int32)[:, None] == col_ids[None, :] // tile_f
    ).astype(jnp.int32)
    picked = jnp.dot(onehot_rows, tile_keys, preferred_element_type=jnp.int32)
    picked = jnp.dot(picked, onehot_cols, preferred_element_type=jnp.int32)
    salt = (
        stream_ids[0] * jnp.int32(mix_one)
        ^ stream_ids[1] * jnp.int32(mix_two)
        ^ stream_ids[2] * jnp.int32(mix_three)
    )
    offset = row_ids[:, None] % tile_t * tile_f + col_ids[None, :] % tile_f
    value = (picked ^ salt) + offset * jnp.int32(golden)
    value = value ^ shift_down(value, 16)
    value = value * jnp.int32(mult_one)
    value = value ^ shift_down(value, 15)
    value = value * jnp.int32(mult_two)
    value = value ^ shift_down(value, 16)
    return (shift_down(value, 8) & jnp.int32(1023) < jnp.int32(922)).astype(f32)


def normal_cdf(value):
    return 0.5 * (1.0 + lax.erf(value * 0.7071067811865476))


def local_gelu(pre, dact, keep):
    scaled = keep * (1.0 / 0.9)
    cdf = normal_cdf(pre)
    act = (pre * cdf * scaled).astype(bf16)
    slope = cdf + pre * jnp.exp(-0.5 * pre * pre) * 0.3989422804014327
    dpre = (dact * scaled * slope).astype(bf16)
    return act, dpre


def near_swap(value):
    return lax.ppermute(value, "col", [(i, i ^ 1) for i in range(16)])


def next_swap(value):
    pairs = []
    for y in range(2):
        for z in range(RING):
            pairs.append((y * RING + z, y * RING + (z + (1 if z % 2 else -1)) % RING))
    return lax.ppermute(value, "col", pairs)


def far_swap(value):
    return lax.ppermute(value, "col", [(i, i ^ 8) for i in range(16)])


def encode(value):
    root = jnp.sqrt(jnp.abs(value) * 262144.0)
    return jnp.where(value < 0, -root, root).astype(jnp.float16)


def decode(code):
    root = code.astype(f32)
    return root * jnp.abs(root) * (1.0 / 262144.0)


def paired(near, back):
    return lax.optimization_barrier((near, back))


def ring_reduce(part):
    half = part(4)
    mid = half.shape[0] // 2
    near, back = paired(near_swap(encode(half[:mid])), next_swap(encode(half[mid:])))
    own = part(5)
    to_next = jnp.concatenate([own[:mid] + decode(near), own[mid:]], 0)
    own = part(3)
    to_near = jnp.concatenate([own[:mid], own[mid:] + decode(back)], 0)
    for k in (2, 1):
        near, back = paired(near_swap(encode(to_near)), next_swap(encode(to_next)))
        to_next = part(8 - k) + decode(near)
        to_near = part(k) + decode(back)
    near = near_swap(encode(to_near))
    back = next_swap(encode(to_next))
    return part(0) + decode(near) + decode(back)


def ring_gather(own, spot):
    height, width = own.shape
    mid = height // 2
    whole = jnp.zeros((8 * height, width), own.dtype)

    def put(whole, chunk, start):
        return lax.dynamic_update_slice(whole, chunk, (start, 0))

    whole = put(whole, own, spot(0))
    near = back = own
    for k in (1, 2, 3):
        near, back = paired(next_swap(near), near_swap(back))
        whole = put(put(whole, back, spot(k)), near, spot(8 - k))
        near, back = back, near
    near, back = near_swap(back[:mid]), next_swap(near[mid:])
    return put(put(whole, near, spot(4)), back, spot(4) + mid)


def row_gather(shard):
    core = lax.axis_index("row") % 2
    mine = jnp.broadcast_to(shard[None], (8,) + shard.shape)
    chips = [[2 * q + c for q in range(8)] for c in range(2)]
    mine = lax.all_to_all(mine, "row", 0, 0, axis_index_groups=chips, tiled=True)
    other = lax.ppermute(mine, "row", [(i, i ^ 1) for i in range(16)])
    height = shard.shape[0] // 2

    def ordered(part):
        near, far = mine[:, part], other[:, part]
        first = jnp.where(core == 0, near, far)
        second = jnp.where(core == 0, far, near)
        return jnp.concatenate([first, second], 1).reshape(16 * height, shard.shape[1])

    return ordered(slice(0, height)), ordered(slice(height, None))


def local(tokens, out_grad, w_in, w_out, bias_in, stream_ids, tile_keys):
    row = lax.axis_index("row")
    col = lax.axis_index("col")
    z = col % RING
    ff = w_in.shape[1]
    width = w_in.shape[0]
    height = tokens.shape[0]
    ahead = jnp.where(z % 2 == 0, 1, -1)

    def spot(k):
        return (z + ahead * k) % RING * (2 * height)

    toks, grads = row_gather(jnp.concatenate([tokens, out_grad], 0))

    pre_terms = encode(jnp.dot(toks, w_in, preferred_element_type=f32))
    dact_terms = encode(
        lax.dot_general(grads, w_out, (((1,), (1,)), ((), ())), preferred_element_type=f32)
    )

    def reduced(terms):
        total = ring_reduce(
            lambda k: decode(lax.dynamic_slice_in_dim(terms, spot(k), 2 * height, 0))
        )
        code = encode(total)
        code, peer = lax.optimization_barrier((code, far_swap(code)))
        return decode(code) + decode(peer)

    pre = reduced(pre_terms) + bias_in[None, :]
    dact = reduced(dact_terms)

    row_ids = spot(0) + jnp.arange(2 * height, dtype=jnp.int32)
    col_ids = row * ff + jnp.arange(ff, dtype=jnp.int32)
    keep = keep_mask(tile_keys, stream_ids, row_ids, col_ids, TILE_T, TILE_F)
    act, dpre = local_gelu(pre, dact, keep)

    dpre_all = ring_gather(dpre, spot)
    act_all = ring_gather(act, spot)

    part = lax.dot_general(
        dpre_all, w_in, (((1,), (1,)), ((), ())), preferred_element_type=f32
    ).astype(bf16)
    part = lax.all_to_all(part.reshape(16, height, width), "row", 0, 0, tiled=True)
    grad_tokens = jnp.sum(part.astype(f32), axis=0).astype(bf16)

    grad_w_in = lax.dot_general(
        toks, dpre_all, (((0,), (0,)), ((), ())), preferred_element_type=f32
    ).astype(bf16)
    grad_w_out = lax.dot_general(
        act_all, grads, (((0,), (0,)), ((), ())), preferred_element_type=f32
    ).astype(bf16)
    grad_bias_in = jnp.sum(dpre_all.astype(f32), axis=0)
    grad_bias_out = jnp.sum(grads.astype(f32), axis=0)
    return (grad_tokens, grad_w_in, grad_w_out, grad_bias_in, grad_bias_out)


def solution(mesh):
    return jax.shard_map(
        local,
        mesh=mesh,
        in_specs=(
            P("row", "col"),
            P("row", "col"),
            P("col", "row"),
            P("row", "col"),
            P("row"),
            P(),
            P(),
        ),
        out_specs=(P("row", "col"), P("col", "row"), P("row", "col"), P("row"), P("col")),
        check_vma=False,
    )
```

```python
import jax
import jax.numpy as jnp
from jax import lax
from jax.sharding import PartitionSpec as P

TILE_T = 8
TILE_F = 128
RING = 8

mix_one = 73856093
mix_two = 19349663
mix_three = 83492791
golden = -1640531535
mult_one = 2146121005
mult_two = -2073254261

f32 = jnp.float32
bf16 = jnp.bfloat16


def shift_down(value, count):
    return lax.shift_right_logical(value, jnp.full(value.shape, count, jnp.int32))


def keep_mask(tile_keys, stream_ids, row_ids, col_ids, tile_t, tile_f):
    onehot_rows = (
        row_ids[:, None] // tile_t == jnp.arange(tile_keys.shape[0], dtype=jnp.int32)[None, :]
    ).astype(jnp.int32)
    onehot_cols = (
        jnp.arange(tile_keys.shape[1], dtype=jnp.int32)[:, None] == col_ids[None, :] // tile_f
    ).astype(jnp.int32)
    picked = jnp.dot(onehot_rows, tile_keys, preferred_element_type=jnp.int32)
    picked = jnp.dot(picked, onehot_cols, preferred_element_type=jnp.int32)
    salt = (
        stream_ids[0] * jnp.int32(mix_one)
        ^ stream_ids[1] * jnp.int32(mix_two)
        ^ stream_ids[2] * jnp.int32(mix_three)
    )
    offset = row_ids[:, None] % tile_t * tile_f + col_ids[None, :] % tile_f
    value = (picked ^ salt) + offset * jnp.int32(golden)
    value = value ^ shift_down(value, 16)
    value = value * jnp.int32(mult_one)
    value = value ^ shift_down(value, 15)
    value = value * jnp.int32(mult_two)
    value = value ^ shift_down(value, 16)
    return (shift_down(value, 8) & jnp.int32(1023) < jnp.int32(922)).astype(f32)


def normal_cdf(value):
    return 0.5 * (1.0 + lax.erf(value * 0.7071067811865476))


def local_gelu(pre, dact, keep):
    scaled = keep * (1.0 / 0.9)
    cdf = normal_cdf(pre)
    act = (pre * cdf * scaled).astype(bf16)
    slope = cdf + pre * jnp.exp(-0.5 * pre * pre) * 0.3989422804014327
    dpre = (dact * scaled * slope).astype(bf16)
    return act, dpre


def near_swap(value):
    return lax.ppermute(value, "col", [(i, i ^ 1) for i in range(16)])


def next_swap(value):
    pairs = []
    for y in range(2):
        for z in range(RING):
            pairs.append((y * RING + z, y * RING + (z + (1 if z % 2 else -1)) % RING))
    return lax.ppermute(value, "col", pairs)


def far_swap(value):
    return lax.ppermute(value, "col", [(i, i ^ 8) for i in range(16)])


def encode(value):
    root = jnp.sqrt(jnp.abs(value) * 262144.0)
    return jnp.where(value < 0, -root, root).astype(jnp.float16)


def decode(code):
    root = code.astype(f32)
    return root * jnp.abs(root) * (1.0 / 262144.0)


def paired(near, back):
    return lax.optimization_barrier((near, back))


def ring_reduce(part):
    half = part(4)
    mid = half.shape[0] // 2
    near, back = paired(near_swap(encode(half[:mid])), next_swap(encode(half[mid:])))
    own = part(5)
    to_next = jnp.concatenate([own[:mid] + decode(near), own[mid:]], 0)
    own = part(3)
    to_near = jnp.concatenate([own[:mid], own[mid:] + decode(back)], 0)
    for k in (2, 1):
        near, back = paired(near_swap(encode(to_near)), next_swap(encode(to_next)))
        to_next = part(8 - k) + decode(near)
        to_near = part(k) + decode(back)
    near = near_swap(encode(to_near))
    back = next_swap(encode(to_next))
    return part(0) + decode(near) + decode(back)


def ring_gather(own, gates):
    mid = own.shape[0] // 2
    chunks = [own] + [None] * 7
    near = back = own
    for k in (1, 2, 3):
        if gates is not None:
            near, back, _ = lax.optimization_barrier((near, back, gates[k]))
        near, back = paired(next_swap(near), near_swap(back))
        chunks[k] = back
        chunks[8 - k] = near
        near, back = back, near
    if gates is not None:
        chunks[4] = near_swap(back)
    else:
        chunks[4] = (near_swap(back[:mid]), next_swap(near[mid:]))
    return chunks


def put(whole, chunk, start):
    return lax.dynamic_update_slice(whole, chunk, (start, 0))


def row_gather(shard):
    core = lax.axis_index("row") % 2
    mine = jnp.broadcast_to(shard[None], (8,) + shard.shape)
    chips = [[2 * q + c for q in range(8)] for c in range(2)]
    mine = lax.all_to_all(mine, "row", 0, 0, axis_index_groups=chips, tiled=True)
    other = lax.ppermute(mine, "row", [(i, i ^ 1) for i in range(16)])
    height = shard.shape[0] // 2

    def ordered(part):
        near, far = mine[:, part], other[:, part]
        first = jnp.where(core == 0, near, far)
        second = jnp.where(core == 0, far, near)
        return jnp.concatenate([first, second], 1).reshape(16 * height, shard.shape[1])

    return ordered(slice(0, height)), ordered(slice(height, None))


def local(tokens, out_grad, w_in, w_out, bias_in, stream_ids, tile_keys):
    row = lax.axis_index("row")
    col = lax.axis_index("col")
    z = col % RING
    ff = w_in.shape[1]
    width = w_in.shape[0]
    height = tokens.shape[0]
    ahead = jnp.where(z % 2 == 0, 1, -1)

    def spot(k):
        return (z + ahead * k) % RING * (2 * height)

    toks, grads = row_gather(jnp.concatenate([tokens, out_grad], 0))

    pre_terms = encode(jnp.dot(toks, w_in, preferred_element_type=f32))
    grads, pre_terms = lax.optimization_barrier((grads, pre_terms))
    dact_terms = encode(
        lax.dot_general(grads, w_out, (((1,), (1,)), ((), ())), preferred_element_type=f32)
    )

    def reduced(terms):
        total = ring_reduce(
            lambda k: decode(lax.dynamic_slice_in_dim(terms, spot(k), 2 * height, 0))
        )
        code = encode(total)
        code, peer = lax.optimization_barrier((code, far_swap(code)))
        return decode(code) + decode(peer)

    pre = reduced(pre_terms) + bias_in[None, :]
    dact = reduced(dact_terms)

    row_ids = spot(0) + jnp.arange(2 * height, dtype=jnp.int32)
    col_ids = row * ff + jnp.arange(ff, dtype=jnp.int32)
    keep = keep_mask(tile_keys, stream_ids, row_ids, col_ids, TILE_T, TILE_F)
    act, dpre = local_gelu(pre, dact, keep)

    dpre_chunks = ring_gather(dpre, None)
    dpre_all = jnp.zeros((16 * height, ff), bf16)
    for k, chunk in enumerate(dpre_chunks):
        if k == 4:
            dpre_all = put(dpre_all, chunk[0], spot(4))
            dpre_all = put(dpre_all, chunk[1], spot(4) + height)
        else:
            dpre_all = put(dpre_all, chunk, spot(k))

    side = col // RING * height
    chunks = ring_gather(lax.dynamic_slice_in_dim(act, side, height, 0), dpre_chunks)
    act_all = put(jnp.zeros((16 * height, ff), bf16), act, spot(0))
    for group in ((1, 7, 2, 6), (3, 5, 4)):
        halves = far_swap(jnp.concatenate([chunks[k] for k in group], 0))
        for i, k in enumerate(group):
            act_all = put(act_all, chunks[k], spot(k) + side)
            half = halves[height * i : height * i + height]
            act_all = put(act_all, half, spot(k) + height - side)

    part = lax.dot_general(
        dpre_all, w_in, (((1,), (1,)), ((), ())), preferred_element_type=f32
    ).astype(bf16)
    part = lax.all_to_all(part.reshape(16, height, width), "row", 0, 0, tiled=True)
    grad_tokens = jnp.sum(part.astype(f32), axis=0).astype(bf16)

    toks, _ = lax.optimization_barrier((toks, chunks[4]))
    grad_w_in = lax.dot_general(
        toks, dpre_all, (((0,), (0,)), ((), ())), preferred_element_type=f32
    ).astype(bf16)
    grad_w_out = lax.dot_general(
        act_all, grads, (((0,), (0,)), ((), ())), preferred_element_type=f32
    ).astype(bf16)
    grad_bias_in = jnp.sum(dpre_all.astype(f32), axis=0)
    grad_bias_out = jnp.sum(grads.astype(f32), axis=0)
    return (grad_tokens, grad_w_in, grad_w_out, grad_bias_in, grad_bias_out)


def solution(mesh):
    return jax.shard_map(
        local,
        mesh=mesh,
        in_specs=(
            P("row", "col"),
            P("row", "col"),
            P("col", "row"),
            P("row", "col"),
            P("row"),
            P(),
            P(),
        ),
        out_specs=(P("row", "col"), P("col", "row"), P("row", "col"), P("row"), P("col")),
        check_vma=False,
    )
```

```python
import jax
import jax.numpy as jnp
from jax import lax
from jax.sharding import PartitionSpec as P

TILE_T = 8
TILE_F = 128
RING = 8

mix_one = 73856093
mix_two = 19349663
mix_three = 83492791
golden = -1640531535
mult_one = 2146121005
mult_two = -2073254261

f32 = jnp.float32
bf16 = jnp.bfloat16


def shift_down(value, count):
    return lax.shift_right_logical(value, jnp.full(value.shape, count, jnp.int32))


def keep_mask(tile_keys, stream_ids, row_ids, col_ids, tile_t, tile_f):
    onehot_rows = (
        row_ids[:, None] // tile_t == jnp.arange(tile_keys.shape[0], dtype=jnp.int32)[None, :]
    ).astype(jnp.int32)
    onehot_cols = (
        jnp.arange(tile_keys.shape[1], dtype=jnp.int32)[:, None] == col_ids[None, :] // tile_f
    ).astype(jnp.int32)
    picked = jnp.dot(onehot_rows, tile_keys, preferred_element_type=jnp.int32)
    picked = jnp.dot(picked, onehot_cols, preferred_element_type=jnp.int32)
    salt = (
        stream_ids[0] * jnp.int32(mix_one)
        ^ stream_ids[1] * jnp.int32(mix_two)
        ^ stream_ids[2] * jnp.int32(mix_three)
    )
    offset = row_ids[:, None] % tile_t * tile_f + col_ids[None, :] % tile_f
    value = (picked ^ salt) + offset * jnp.int32(golden)
    value = value ^ shift_down(value, 16)
    value = value * jnp.int32(mult_one)
    value = value ^ shift_down(value, 15)
    value = value * jnp.int32(mult_two)
    value = value ^ shift_down(value, 16)
    return (shift_down(value, 8) & jnp.int32(1023) < jnp.int32(922)).astype(f32)


def normal_cdf(value):
    return 0.5 * (1.0 + lax.erf(value * 0.7071067811865476))


def local_gelu(pre, dact, keep):
    scaled = keep * (1.0 / 0.9)
    cdf = normal_cdf(pre)
    act = (pre * cdf * scaled).astype(bf16)
    slope = cdf + pre * jnp.exp(-0.5 * pre * pre) * 0.3989422804014327
    dpre = (dact * scaled * slope).astype(bf16)
    return act, dpre


def near_swap(value):
    return lax.ppermute(value, "col", [(i, i ^ 1) for i in range(16)])


def next_swap(value):
    pairs = []
    for y in range(2):
        for z in range(RING):
            pairs.append((y * RING + z, y * RING + (z + (1 if z % 2 else -1)) % RING))
    return lax.ppermute(value, "col", pairs)


def far_swap(value):
    return lax.ppermute(value, "col", [(i, i ^ 8) for i in range(16)])


def encode(value):
    root = jnp.sqrt(jnp.abs(value) * 262144.0)
    return jnp.where(value < 0, -root, root).astype(jnp.float16)


def decode(code):
    root = code.astype(f32)
    return root * jnp.abs(root) * (1.0 / 262144.0)


def paired(near, back):
    return lax.optimization_barrier((near, back))


def ring_reduce(part):
    half = part(4)
    mid = half.shape[0] // 2
    near, back = paired(near_swap(encode(half[:mid])), next_swap(encode(half[mid:])))
    own = part(5)
    to_next = jnp.concatenate([own[:mid] + decode(near), own[mid:]], 0)
    own = part(3)
    to_near = jnp.concatenate([own[:mid], own[mid:] + decode(back)], 0)
    for k in (2, 1):
        near, back = paired(near_swap(encode(to_near)), next_swap(encode(to_next)))
        to_next = part(8 - k) + decode(near)
        to_near = part(k) + decode(back)
    near = near_swap(encode(to_near))
    back = next_swap(encode(to_next))
    return part(0) + decode(near) + decode(back)


def ring_gather(own, spot):
    height, width = own.shape
    mid = height // 2
    whole = jnp.zeros((8 * height, width), own.dtype)

    def put(whole, chunk, start):
        return lax.dynamic_update_slice(whole, chunk, (start, 0))

    whole = put(whole, own, spot(0))
    near = back = own
    for k in (1, 2, 3):
        near, back = paired(next_swap(near), near_swap(back))
        whole = put(put(whole, back, spot(k)), near, spot(8 - k))
        near, back = back, near
    near, back = near_swap(back[:mid]), next_swap(near[mid:])
    return put(put(whole, near, spot(4)), back, spot(4) + mid)


def row_gather(shard):
    core = lax.axis_index("row") % 2
    mine = jnp.broadcast_to(shard[None], (8,) + shard.shape)
    chips = [[2 * q + c for q in range(8)] for c in range(2)]
    mine = lax.all_to_all(mine, "row", 0, 0, axis_index_groups=chips, tiled=True)
    other = lax.ppermute(mine, "row", [(i, i ^ 1) for i in range(16)])
    height = shard.shape[0] // 2

    def ordered(part):
        near, far = mine[:, part], other[:, part]
        first = jnp.where(core == 0, near, far)
        second = jnp.where(core == 0, far, near)
        return jnp.concatenate([first, second], 1).reshape(16 * height, shard.shape[1])

    return ordered(slice(0, height)), ordered(slice(height, None))


def local(tokens, out_grad, w_in, w_out, bias_in, stream_ids, tile_keys):
    row = lax.axis_index("row")
    col = lax.axis_index("col")
    z = col % RING
    ff = w_in.shape[1]
    width = w_in.shape[0]
    height = tokens.shape[0]
    ahead = jnp.where(z % 2 == 0, 1, -1)

    def spot(k):
        return (z + ahead * k) % RING * (2 * height)

    toks, grads = row_gather(jnp.concatenate([tokens, out_grad], 0))

    pre_terms = encode(jnp.dot(toks, w_in, preferred_element_type=f32))
    grads, pre_terms = lax.optimization_barrier((grads, pre_terms))
    dact_terms = encode(
        lax.dot_general(grads, w_out, (((1,), (1,)), ((), ())), preferred_element_type=f32)
    )

    def reduced(terms):
        total = ring_reduce(
            lambda k: decode(lax.dynamic_slice_in_dim(terms, spot(k), 2 * height, 0))
        )
        code = encode(total)
        code, peer = lax.optimization_barrier((code, far_swap(code)))
        return decode(code) + decode(peer)

    pre = reduced(pre_terms) + bias_in[None, :]
    dact = reduced(dact_terms)

    row_ids = spot(0) + jnp.arange(2 * height, dtype=jnp.int32)
    col_ids = row * ff + jnp.arange(ff, dtype=jnp.int32)
    keep = keep_mask(tile_keys, stream_ids, row_ids, col_ids, TILE_T, TILE_F)
    act, dpre = local_gelu(pre, dact, keep)

    act, dpre = lax.optimization_barrier((act, dpre))
    dpre_all = ring_gather(dpre, spot)
    act_all = ring_gather(act, spot)

    part = lax.dot_general(
        dpre_all, w_in, (((1,), (1,)), ((), ())), preferred_element_type=f32
    ).astype(bf16)
    part = lax.all_to_all(part.reshape(16, height, width), "row", 0, 0, tiled=True)
    grad_tokens = jnp.sum(part.astype(f32), axis=0).astype(bf16)

    grad_w_in = lax.dot_general(
        toks, dpre_all, (((0,), (0,)), ((), ())), preferred_element_type=f32
    ).astype(bf16)
    grad_w_out = lax.dot_general(
        act_all, grads, (((0,), (0,)), ((), ())), preferred_element_type=f32
    ).astype(bf16)
    grad_bias_in = jnp.sum(dpre_all.astype(f32), axis=0)
    grad_bias_out = jnp.sum(grads.astype(f32), axis=0)
    return (grad_tokens, grad_w_in, grad_w_out, grad_bias_in, grad_bias_out)


def solution(mesh):
    return jax.shard_map(
        local,
        mesh=mesh,
        in_specs=(
            P("row", "col"),
            P("row", "col"),
            P("col", "row"),
            P("row", "col"),
            P("row"),
            P(),
            P(),
        ),
        out_specs=(P("row", "col"), P("col", "row"), P("row", "col"), P("row"), P("col")),
        check_vma=False,
    )
```

```python
import jax
import jax.numpy as jnp
from jax import lax
from jax.sharding import PartitionSpec as P

TILE_T = 8
TILE_F = 128
RING = 8

mix_one = 73856093
mix_two = 19349663
mix_three = 83492791
golden = -1640531535
mult_one = 2146121005
mult_two = -2073254261

f32 = jnp.float32
bf16 = jnp.bfloat16


def shift_down(value, count):
    return lax.shift_right_logical(value, jnp.full(value.shape, count, jnp.int32))


def keep_mask(tile_keys, stream_ids, row_ids, col_ids, tile_t, tile_f):
    onehot_rows = (
        row_ids[:, None] // tile_t == jnp.arange(tile_keys.shape[0], dtype=jnp.int32)[None, :]
    ).astype(jnp.int32)
    onehot_cols = (
        jnp.arange(tile_keys.shape[1], dtype=jnp.int32)[:, None] == col_ids[None, :] // tile_f
    ).astype(jnp.int32)
    picked = jnp.dot(onehot_rows, tile_keys, preferred_element_type=jnp.int32)
    picked = jnp.dot(picked, onehot_cols, preferred_element_type=jnp.int32)
    salt = (
        stream_ids[0] * jnp.int32(mix_one)
        ^ stream_ids[1] * jnp.int32(mix_two)
        ^ stream_ids[2] * jnp.int32(mix_three)
    )
    offset = row_ids[:, None] % tile_t * tile_f + col_ids[None, :] % tile_f
    value = (picked ^ salt) + offset * jnp.int32(golden)
    value = value ^ shift_down(value, 16)
    value = value * jnp.int32(mult_one)
    value = value ^ shift_down(value, 15)
    value = value * jnp.int32(mult_two)
    value = value ^ shift_down(value, 16)
    return (shift_down(value, 8) & jnp.int32(1023) < jnp.int32(922)).astype(f32)


def normal_cdf(value):
    return 0.5 * (1.0 + lax.erf(value * 0.7071067811865476))


def local_gelu(pre, dact, keep):
    scaled = keep * (1.0 / 0.9)
    cdf = normal_cdf(pre)
    act = (pre * cdf * scaled).astype(bf16)
    slope = cdf + pre * jnp.exp(-0.5 * pre * pre) * 0.3989422804014327
    dpre = (dact * scaled * slope).astype(bf16)
    return act, dpre


def ring_pairs(flip):
    pairs = []
    for r in range(16):
        for c in range(16):
            step = 1 if (r + c + flip) % 2 == 0 else -1
            pairs.append((r * 16 + c, r * 16 + c // RING * RING + (c + step) % RING))
    return pairs


def near_swap(value):
    return lax.ppermute(value, ("row", "col"), ring_pairs(0))


def next_swap(value):
    return lax.ppermute(value, ("row", "col"), ring_pairs(1))


def far_swap(value):
    return lax.ppermute(value, "col", [(i, i ^ 8) for i in range(16)])


def encode(value):
    root = jnp.sqrt(jnp.abs(value) * 262144.0)
    return jnp.where(value < 0, -root, root).astype(jnp.float16)


def decode(code):
    root = code.astype(f32)
    return root * jnp.abs(root) * (1.0 / 262144.0)


def paired(near, back):
    return lax.optimization_barrier((near, back))


def ring_reduce(part):
    half = part(4)
    mid = half.shape[0] // 2
    near, back = paired(near_swap(encode(half[:mid])), next_swap(encode(half[mid:])))
    own = part(5)
    to_next = jnp.concatenate([own[:mid] + decode(near), own[mid:]], 0)
    own = part(3)
    to_near = jnp.concatenate([own[:mid], own[mid:] + decode(back)], 0)
    for k in (2, 1):
        near, back = paired(near_swap(encode(to_near)), next_swap(encode(to_next)))
        to_next = part(8 - k) + decode(near)
        to_near = part(k) + decode(back)
    near = near_swap(encode(to_near))
    back = next_swap(encode(to_next))
    return part(0) + decode(near) + decode(back)


def ring_gather(own, spot):
    height, width = own.shape
    mid = height // 2
    whole = jnp.zeros((8 * height, width), own.dtype)

    def put(whole, chunk, start):
        return lax.dynamic_update_slice(whole, chunk, (start, 0))

    whole = put(whole, own, spot(0))
    near = back = own
    for k in (1, 2, 3):
        near, back = paired(next_swap(near), near_swap(back))
        whole = put(put(whole, back, spot(k)), near, spot(8 - k))
        near, back = back, near
    near, back = near_swap(back[:mid]), next_swap(near[mid:])
    return put(put(whole, near, spot(4)), back, spot(4) + mid)


def row_gather(shard):
    core = lax.axis_index("row") % 2
    mine = jnp.broadcast_to(shard[None], (8,) + shard.shape)
    chips = [[2 * q + c for q in range(8)] for c in range(2)]
    mine = lax.all_to_all(mine, "row", 0, 0, axis_index_groups=chips, tiled=True)
    other = lax.ppermute(mine, "row", [(i, i ^ 1) for i in range(16)])
    height = shard.shape[0] // 2

    def ordered(part):
        near, far = mine[:, part], other[:, part]
        first = jnp.where(core == 0, near, far)
        second = jnp.where(core == 0, far, near)
        return jnp.concatenate([first, second], 1).reshape(16 * height, shard.shape[1])

    return ordered(slice(0, height)), ordered(slice(height, None))


def local(tokens, out_grad, w_in, w_out, bias_in, stream_ids, tile_keys):
    row = lax.axis_index("row")
    col = lax.axis_index("col")
    z = col % RING
    ff = w_in.shape[1]
    width = w_in.shape[0]
    height = tokens.shape[0]
    ahead = jnp.where((row + z) % 2 == 0, 1, -1)

    def spot(k):
        return (z + ahead * k) % RING * (2 * height)

    toks, grads = row_gather(jnp.concatenate([tokens, out_grad], 0))

    pre_terms = encode(jnp.dot(toks, w_in, preferred_element_type=f32))
    grads, pre_terms = lax.optimization_barrier((grads, pre_terms))
    dact_terms = encode(
        lax.dot_general(grads, w_out, (((1,), (1,)), ((), ())), preferred_element_type=f32)
    )

    def reduced(terms):
        total = ring_reduce(
            lambda k: decode(lax.dynamic_slice_in_dim(terms, spot(k), 2 * height, 0))
        )
        code = encode(total)
        code, peer = lax.optimization_barrier((code, far_swap(code)))
        return decode(code) + decode(peer)

    pre = reduced(pre_terms) + bias_in[None, :]
    dact = reduced(dact_terms)

    row_ids = spot(0) + jnp.arange(2 * height, dtype=jnp.int32)
    col_ids = row * ff + jnp.arange(ff, dtype=jnp.int32)
    keep = keep_mask(tile_keys, stream_ids, row_ids, col_ids, TILE_T, TILE_F)
    act, dpre = local_gelu(pre, dact, keep)

    act, dpre = lax.optimization_barrier((act, dpre))
    dpre_all = ring_gather(dpre, spot)
    act_all = ring_gather(act, spot)

    part = lax.dot_general(
        dpre_all, w_in, (((1,), (1,)), ((), ())), preferred_element_type=f32
    ).astype(bf16)
    part = lax.all_to_all(part.reshape(16, height, width), "row", 0, 0, tiled=True)
    grad_tokens = jnp.sum(part.astype(f32), axis=0).astype(bf16)

    grad_w_in = lax.dot_general(
        toks, dpre_all, (((0,), (0,)), ((), ())), preferred_element_type=f32
    ).astype(bf16)
    grad_w_out = lax.dot_general(
        act_all, grads, (((0,), (0,)), ((), ())), preferred_element_type=f32
    ).astype(bf16)
    grad_bias_in = jnp.sum(dpre_all.astype(f32), axis=0)
    grad_bias_out = jnp.sum(grads.astype(f32), axis=0)
    return (grad_tokens, grad_w_in, grad_w_out, grad_bias_in, grad_bias_out)


def solution(mesh):
    return jax.shard_map(
        local,
        mesh=mesh,
        in_specs=(
            P("row", "col"),
            P("row", "col"),
            P("col", "row"),
            P("row", "col"),
            P("row"),
            P(),
            P(),
        ),
        out_specs=(P("row", "col"), P("col", "row"), P("row", "col"), P("row"), P("col")),
        check_vma=False,
    )
```

```python
import jax
import jax.numpy as jnp
from jax import lax
from jax.sharding import PartitionSpec as P

TILE_T = 8
TILE_F = 128
RING = 8

mix_one = 73856093
mix_two = 19349663
mix_three = 83492791
golden = -1640531535
mult_one = 2146121005
mult_two = -2073254261

f32 = jnp.float32
bf16 = jnp.bfloat16


def shift_down(value, count):
    return lax.shift_right_logical(value, jnp.full(value.shape, count, jnp.int32))


def keep_mask(tile_keys, stream_ids, row_ids, col_ids, tile_t, tile_f):
    onehot_rows = (
        row_ids[:, None] // tile_t == jnp.arange(tile_keys.shape[0], dtype=jnp.int32)[None, :]
    ).astype(jnp.int32)
    onehot_cols = (
        jnp.arange(tile_keys.shape[1], dtype=jnp.int32)[:, None] == col_ids[None, :] // tile_f
    ).astype(jnp.int32)
    picked = jnp.dot(onehot_rows, tile_keys, preferred_element_type=jnp.int32)
    picked = jnp.dot(picked, onehot_cols, preferred_element_type=jnp.int32)
    salt = (
        stream_ids[0] * jnp.int32(mix_one)
        ^ stream_ids[1] * jnp.int32(mix_two)
        ^ stream_ids[2] * jnp.int32(mix_three)
    )
    offset = row_ids[:, None] % tile_t * tile_f + col_ids[None, :] % tile_f
    value = (picked ^ salt) + offset * jnp.int32(golden)
    value = value ^ shift_down(value, 16)
    value = value * jnp.int32(mult_one)
    value = value ^ shift_down(value, 15)
    value = value * jnp.int32(mult_two)
    value = value ^ shift_down(value, 16)
    return (shift_down(value, 8) & jnp.int32(1023) < jnp.int32(922)).astype(f32)


def normal_cdf(value):
    return 0.5 * (1.0 + lax.erf(value * 0.7071067811865476))


def local_gelu(pre, dact, keep):
    scaled = keep * (1.0 / 0.9)
    cdf = normal_cdf(pre)
    act = (pre * cdf * scaled).astype(bf16)
    slope = cdf + pre * jnp.exp(-0.5 * pre * pre) * 0.3989422804014327
    dpre = (dact * scaled * slope).astype(bf16)
    return act, dpre


def near_swap(value):
    return lax.ppermute(value, "col", [(i, i ^ 1) for i in range(16)])


def next_swap(value):
    pairs = []
    for y in range(2):
        for z in range(RING):
            pairs.append((y * RING + z, y * RING + (z + (1 if z % 2 else -1)) % RING))
    return lax.ppermute(value, "col", pairs)


def far_swap(value):
    return lax.ppermute(value, "col", [(i, i ^ 8) for i in range(16)])


def encode(value):
    root = jnp.sqrt(jnp.abs(value) * 262144.0)
    return jnp.where(value < 0, -root, root).astype(jnp.float16)


def decode(code):
    root = code.astype(f32)
    return root * jnp.abs(root) * (1.0 / 262144.0)


def paired(near, back):
    return lax.optimization_barrier((near, back))


def ring_reduce(part):
    half = part(4)
    mid = half.shape[0] // 2
    near, back = paired(near_swap(encode(half[:mid])), next_swap(encode(half[mid:])))
    first = near
    own = part(5)
    to_next = jnp.concatenate([own[:mid] + decode(near), own[mid:]], 0)
    own = part(3)
    to_near = jnp.concatenate([own[:mid], own[mid:] + decode(back)], 0)
    for k in (2, 1):
        near, back = paired(near_swap(encode(to_near)), next_swap(encode(to_next)))
        to_next = part(8 - k) + decode(near)
        to_near = part(k) + decode(back)
    near = near_swap(encode(to_near))
    back = next_swap(encode(to_next))
    return part(0) + decode(near) + decode(back), first


def ring_gather(own, spot):
    height, width = own.shape
    mid = height // 2
    whole = jnp.zeros((8 * height, width), own.dtype)

    def put(whole, chunk, start):
        return lax.dynamic_update_slice(whole, chunk, (start, 0))

    whole = put(whole, own, spot(0))
    near = back = own
    for k in (1, 2, 3):
        near, back = paired(next_swap(near), near_swap(back))
        whole = put(put(whole, back, spot(k)), near, spot(8 - k))
        near, back = back, near
    near, back = near_swap(back[:mid]), next_swap(near[mid:])
    return put(put(whole, near, spot(4)), back, spot(4) + mid)


def row_gather(shard):
    height, width = shard.shape
    core = lax.axis_index("row") % 2
    mine = jnp.broadcast_to(shard[None], (8, height, width))
    chips = [[2 * q + c for q in range(8)] for c in range(2)]
    mine = lax.all_to_all(mine, "row", 0, 0, axis_index_groups=chips, tiled=True)
    other = lax.ppermute(mine, "row", [(i, i ^ 1) for i in range(16)])
    first = jnp.where(core == 0, mine, other)
    second = jnp.where(core == 0, other, mine)
    return jnp.concatenate([first, second], 1).reshape(16 * height, width)


def row_gather_at_once(shard):
    height, width = shard.shape
    whole = jnp.broadcast_to(shard[None], (16, height, width))
    whole = lax.all_to_all(whole, "row", 0, 0, tiled=True)
    return whole.reshape(16 * height, width)


def local(tokens, out_grad, w_in, w_out, bias_in, stream_ids, tile_keys):
    row = lax.axis_index("row")
    col = lax.axis_index("col")
    z = col % RING
    ff = w_in.shape[1]
    width = w_in.shape[0]
    height = tokens.shape[0]
    ahead = jnp.where(z % 2 == 0, 1, -1)

    def spot(k):
        return (z + ahead * k) % RING * (2 * height)

    toks = row_gather(tokens)
    grads = row_gather_at_once(out_grad)

    def reduced(terms):
        total, first = ring_reduce(
            lambda k: decode(lax.dynamic_slice_in_dim(terms, spot(k), 2 * height, 0))
        )
        code = encode(total)
        code, peer = lax.optimization_barrier((code, far_swap(code)))
        return decode(code) + decode(peer), first

    pre, first = reduced(encode(jnp.dot(toks, w_in, preferred_element_type=f32)))
    pre = pre + bias_in[None, :]
    grads, _ = lax.optimization_barrier((grads, first))
    dact, _ = reduced(
        encode(lax.dot_general(grads, w_out, (((1,), (1,)), ((), ())), preferred_element_type=f32))
    )

    row_ids = spot(0) + jnp.arange(2 * height, dtype=jnp.int32)
    col_ids = row * ff + jnp.arange(ff, dtype=jnp.int32)
    keep = keep_mask(tile_keys, stream_ids, row_ids, col_ids, TILE_T, TILE_F)
    act, dpre = local_gelu(pre, dact, keep)

    act, dpre = lax.optimization_barrier((act, dpre))
    dpre_all = ring_gather(dpre, spot)
    act_all = ring_gather(act, spot)

    part = lax.dot_general(
        dpre_all, w_in, (((1,), (1,)), ((), ())), preferred_element_type=f32
    ).astype(bf16)
    part = lax.all_to_all(part.reshape(16, height, width), "row", 0, 0, tiled=True)
    grad_tokens = jnp.sum(part.astype(f32), axis=0).astype(bf16)

    grad_w_in = lax.dot_general(
        toks, dpre_all, (((0,), (0,)), ((), ())), preferred_element_type=f32
    ).astype(bf16)
    grad_w_out = lax.dot_general(
        act_all, grads, (((0,), (0,)), ((), ())), preferred_element_type=f32
    ).astype(bf16)
    grad_bias_in = jnp.sum(dpre_all.astype(f32), axis=0)
    grad_bias_out = jnp.sum(grads.astype(f32), axis=0)
    return (grad_tokens, grad_w_in, grad_w_out, grad_bias_in, grad_bias_out)


def solution(mesh):
    return jax.shard_map(
        local,
        mesh=mesh,
        in_specs=(
            P("row", "col"),
            P("row", "col"),
            P("col", "row"),
            P("row", "col"),
            P("row"),
            P(),
            P(),
        ),
        out_specs=(P("row", "col"), P("col", "row"), P("row", "col"), P("row"), P("col")),
        check_vma=False,
    )
```

```python
import jax
import jax.numpy as jnp
from jax import lax
from jax.sharding import PartitionSpec as P

TILE_T = 8
TILE_F = 128
RING = 8

mix_one = 73856093
mix_two = 19349663
mix_three = 83492791
golden = -1640531535
mult_one = 2146121005
mult_two = -2073254261

f32 = jnp.float32
bf16 = jnp.bfloat16


def shift_down(value, count):
    return lax.shift_right_logical(value, jnp.full(value.shape, count, jnp.int32))


def keep_mask(tile_keys, stream_ids, row_ids, col_ids, tile_t, tile_f):
    onehot_rows = (
        row_ids[:, None] // tile_t == jnp.arange(tile_keys.shape[0], dtype=jnp.int32)[None, :]
    ).astype(jnp.int32)
    onehot_cols = (
        jnp.arange(tile_keys.shape[1], dtype=jnp.int32)[:, None] == col_ids[None, :] // tile_f
    ).astype(jnp.int32)
    picked = jnp.dot(onehot_rows, tile_keys, preferred_element_type=jnp.int32)
    picked = jnp.dot(picked, onehot_cols, preferred_element_type=jnp.int32)
    salt = (
        stream_ids[0] * jnp.int32(mix_one)
        ^ stream_ids[1] * jnp.int32(mix_two)
        ^ stream_ids[2] * jnp.int32(mix_three)
    )
    offset = row_ids[:, None] % tile_t * tile_f + col_ids[None, :] % tile_f
    value = (picked ^ salt) + offset * jnp.int32(golden)
    value = value ^ shift_down(value, 16)
    value = value * jnp.int32(mult_one)
    value = value ^ shift_down(value, 15)
    value = value * jnp.int32(mult_two)
    value = value ^ shift_down(value, 16)
    return (shift_down(value, 8) & jnp.int32(1023) < jnp.int32(922)).astype(f32)


def normal_cdf(value):
    return 0.5 * (1.0 + lax.erf(value * 0.7071067811865476))


def local_gelu(pre, dact, keep):
    scaled = keep * (1.0 / 0.9)
    cdf = normal_cdf(pre)
    act = (pre * cdf * scaled).astype(bf16)
    slope = cdf + pre * jnp.exp(-0.5 * pre * pre) * 0.3989422804014327
    dpre = (dact * scaled * slope).astype(bf16)
    return act, dpre


def near_swap(value):
    return lax.ppermute(value, "col", [(i, i ^ 1) for i in range(16)])


def next_swap(value):
    pairs = []
    for y in range(2):
        for z in range(RING):
            pairs.append((y * RING + z, y * RING + (z + (1 if z % 2 else -1)) % RING))
    return lax.ppermute(value, "col", pairs)


def far_swap(value):
    return lax.ppermute(value, "col", [(i, i ^ 8) for i in range(16)])


def encode(value):
    root = jnp.sqrt(jnp.abs(value) * 262144.0)
    return jnp.where(value < 0, -root, root).astype(jnp.float16)


def decode(code):
    root = code.astype(f32)
    return root * jnp.abs(root) * (1.0 / 262144.0)


def paired(near, back):
    return lax.optimization_barrier((near, back))


def ring_reduce(part):
    half = part(4)
    mid = half.shape[0] // 2
    near, back = paired(near_swap(encode(half[:mid])), next_swap(encode(half[mid:])))
    first = near
    own = part(5)
    to_next = jnp.concatenate([own[:mid] + decode(near), own[mid:]], 0)
    own = part(3)
    to_near = jnp.concatenate([own[:mid], own[mid:] + decode(back)], 0)
    for k in (2, 1):
        near, back = paired(near_swap(encode(to_near)), next_swap(encode(to_next)))
        to_next = part(8 - k) + decode(near)
        to_near = part(k) + decode(back)
    near = near_swap(encode(to_near))
    back = next_swap(encode(to_next))
    return part(0) + decode(near) + decode(back), first


def ring_gather(own, spot):
    height, width = own.shape
    mid = height // 2
    whole = jnp.zeros((8 * height, width), own.dtype)

    def put(whole, chunk, start):
        return lax.dynamic_update_slice(whole, chunk, (start, 0))

    whole = put(whole, own, spot(0))
    near = back = own
    for k in (1, 2, 3):
        near, back = paired(next_swap(near), near_swap(back))
        whole = put(put(whole, back, spot(k)), near, spot(8 - k))
        near, back = back, near
    near, back = near_swap(back[:mid]), next_swap(near[mid:])
    return put(put(whole, near, spot(4)), back, spot(4) + mid)


def row_gather(*shards):
    core = lax.axis_index("row") % 2
    packed = jnp.concatenate(shards, 0)
    mine = jnp.broadcast_to(packed[None], (8,) + packed.shape)
    chips = [[2 * q + c for q in range(8)] for c in range(2)]
    mine = lax.all_to_all(mine, "row", 0, 0, axis_index_groups=chips, tiled=True)
    other = lax.ppermute(mine, "row", [(i, i ^ 1) for i in range(16)])
    height, width = shards[0].shape

    def ordered(part):
        near, far = mine[:, part], other[:, part]
        first = jnp.where(core == 0, near, far)
        second = jnp.where(core == 0, far, near)
        return jnp.concatenate([first, second], 1).reshape(16 * height, width)

    return ordered(slice(0, height)), ordered(slice(height, None))


def local(tokens, out_grad, w_in, w_out, bias_in, stream_ids, tile_keys):
    row = lax.axis_index("row")
    col = lax.axis_index("col")
    z = col % RING
    ff = w_in.shape[1]
    width = w_in.shape[0]
    height = tokens.shape[0]
    ahead = jnp.where(z % 2 == 0, 1, -1)

    def spot(k):
        return (z + ahead * k) % RING * (2 * height)

    toks, grads = row_gather(tokens, out_grad)

    pre_terms = encode(jnp.dot(toks, w_in, preferred_element_type=f32))
    grads, pre_terms = lax.optimization_barrier((grads, pre_terms))
    dact_terms = encode(
        lax.dot_general(grads, w_out, (((1,), (1,)), ((), ())), preferred_element_type=f32)
    )

    def reduced(terms):
        total, first = ring_reduce(
            lambda k: decode(lax.dynamic_slice_in_dim(terms, spot(k), 2 * height, 0))
        )
        code = encode(total)
        code, peer = lax.optimization_barrier((code, far_swap(code)))
        return decode(code) + decode(peer), first

    pre, first = reduced(pre_terms)
    pre = pre + bias_in[None, :]
    dact, _ = reduced(dact_terms)

    top, side, stream_ids, _ = lax.optimization_barrier((spot(0), row * ff, stream_ids, first))
    row_ids = top + jnp.arange(2 * height, dtype=jnp.int32)
    col_ids = side + jnp.arange(ff, dtype=jnp.int32)
    keep = keep_mask(tile_keys, stream_ids, row_ids, col_ids, TILE_T, TILE_F)
    act, dpre = local_gelu(pre, dact, keep)

    act, dpre = lax.optimization_barrier((act, dpre))
    dpre_all = ring_gather(dpre, spot)
    act_all = ring_gather(act, spot)

    part = lax.dot_general(
        dpre_all, w_in, (((1,), (1,)), ((), ())), preferred_element_type=f32
    ).astype(bf16)
    part = lax.all_to_all(part.reshape(16, height, width), "row", 0, 0, tiled=True)
    grad_tokens = jnp.sum(part.astype(f32), axis=0).astype(bf16)

    grad_w_in = lax.dot_general(
        toks, dpre_all, (((0,), (0,)), ((), ())), preferred_element_type=f32
    ).astype(bf16)
    grad_w_out = lax.dot_general(
        act_all, grads, (((0,), (0,)), ((), ())), preferred_element_type=f32
    ).astype(bf16)
    grad_bias_in = jnp.sum(dpre_all.astype(f32), axis=0)
    grad_bias_out = jnp.sum(grads.astype(f32), axis=0)
    return (grad_tokens, grad_w_in, grad_w_out, grad_bias_in, grad_bias_out)


def solution(mesh):
    return jax.shard_map(
        local,
        mesh=mesh,
        in_specs=(
            P("row", "col"),
            P("row", "col"),
            P("col", "row"),
            P("row", "col"),
            P("row"),
            P(),
            P(),
        ),
        out_specs=(P("row", "col"), P("col", "row"), P("row", "col"), P("row"), P("col")),
        check_vma=False,
    )
```
